256 devices in a mesh: grp: 32 (over y, x, core), own: 8 (over z).
Axes of the slice: x: 4, y: 4, z: 8, core: 2. Of those that a mesh axis runs over, the one named last changes fastest.
Arguments:
- embeddings: bfloat16 [2048, 32, 1024], P(('grp', 'own')), may hold values from -16 to 16
- cluster_ids: int32 [2048, 32], P(('grp', 'own')), may hold values from 0 to 3
- owners: int32 [2048, 1], P(('grp', 'own')), may hold values from 0 to 7; in each aligned block of 8 rows (0 to 7, 8 to 15, ...) at most 2 rows name the same one
- pattern: int32 [32, 32], replicated, may hold values 0 or 1
Outputs:
- best: float32 [2048, 32], P(('grp', 'own'))
The draws below stay inside these ranges and needn't reach their ends.
Inputs may be any that keep to these rules, and one draw needn't show every extreme that they name: `owners`: A device sends at most 2 tiles to one owner; some device sends exactly 2 tiles to one owner.
All inputs are finite; a program needn't handle non-finite values.
Results may differ from the reference program's by a relative error of at most 0.00057.
Values may be sent and summed in bfloat16 or wider, within the bound.
No kernel may reach another device: no remote copies, remote signals or barrier semaphores. Data moves between devices by JAX's collectives and lax.ppermute only.
A program may use at most 64 MiB of HBM per device.

```python
import math
import jax
import jax.numpy as jnp
import numpy as np
from jax import lax

D = 1024
TILE_ROWS = 32
TILES_DEV = 8
CAPACITY = 2
CLUSTERS = 4
TILES = 2048
N_GRP = 32
N_OWN = 8


def draw_embeddings(key, part):
    topics = max(TILES * TILE_ROWS // 16, 1)
    key_table, key_which, key_strength, key_noise = jax.random.split(key, 4)
    table = jax.random.normal(key_table, (topics, D), jnp.float32)
    which = jax.random.randint(key_which, (TILES, TILE_ROWS), 0, topics)
    strength = jnp.exp(jax.random.uniform(key_strength, (TILES, TILE_ROWS, 1), jnp.float32, math.log(0.3), math.log(3.0)))
    noise = jax.random.normal(key_noise, (TILES, TILE_ROWS, D), jnp.float32)
    values = noise + strength * table[which]
    return jnp.clip(values, -16.0, 16.0).astype(jnp.bfloat16)


def with_ends(entries, rng, smallest, top_value):
    place = [jax.random.randint(jax.random.fold_in(rng, axis), (), 0, length) for axis, length in enumerate(entries.shape)]
    longest = entries.shape.index(max(entries.shape))
    neighbour = place[:longest] + [(place[longest] + 1) % entries.shape[longest]] + place[longest + 1:]
    return entries.at[tuple(place)].set(smallest).at[tuple(neighbour)].set(top_value)


def deal_out(stream_key, own, number, rows, number_of, top, most, slope):
    order = jax.random.permutation(stream_key, number_of)
    crowded, common = portions_of(number_of, rows * top, most, slope, True), portions_of(number_of, rows * top, most, slope, False)
    places = jnp.arange(number_of)

    def named(lengths, turn):
        used = int((lengths > 0).sum())
        fixed = max(1, used // 4)
        shifted = fixed + (places - fixed + turn * (used - fixed)) % max(1, number_of - fixed)
        return jnp.zeros((number_of,), jnp.int32).at[order[jnp.where(places < fixed, places, shifted)]].set(jnp.asarray(lengths, jnp.int32))

    lengths = jnp.where(number % 4 == 0, named(crowded, number // 4), named(common, number - number // 4 - 1))
    mixed = jax.random.permutation(jax.random.fold_in(own, 3), number_of)
    source_of, taker = mixed[0:number_of // 2 * 2:2], mixed[1:number_of // 2 * 2:2]
    slack = jnp.minimum(lengths[source_of] - 1, most - lengths[taker]) // 2
    slack = jnp.where((source_of == order[0]) | (taker == order[0]) | (lengths[taker] == 0), 0, jnp.maximum(slack, 0))
    shifted = jax.random.randint(jax.random.fold_in(own, 4), (number_of // 2,), 0, 1 << 20) % (slack + 1)
    lengths = lengths.at[source_of].add(-shifted).at[taker].add(shifted)
    labels = jnp.searchsorted(jnp.cumsum(lengths), jnp.arange(rows * top), side="right").astype(jnp.int32)
    grid = labels.reshape(top, rows).T
    grid = grid[jax.random.permutation(jax.random.fold_in(own, 1), rows)]
    turn = jax.random.randint(jax.random.fold_in(own, 2), (rows, 1), 0, top)
    return jnp.take_along_axis(grid, (jnp.arange(top)[None, :] + turn) % top, axis=1)


def portions_of(count, total, reach, slope, full):
    portions = [(1 << 20) // math.isqrt(rank ** slope) + 1 for rank in range(1, count + 1)]
    largest = reach if full else min(reach, max(-(-total // count), total * portions[0] // sum(portions)))
    least = 1 if total - largest >= count - 1 else 0
    given, spare = [largest] + [least] * (count - 1), total - largest - least * (count - 1)
    while spare > 0:
        free = [i for i in range(1, count) if given[i] < largest] or [i for i in range(1, count) if given[i] < reach]
        whole, left = sum([portions[i] for i in free]), spare
        for i in free:
            more = min(reach - given[i], max(1, left * portions[i] // whole), spare)
            given[i] = given[i] + more
            spare = spare - more
    return np.array(given)


def setup_inputs(seed: int = 0) -> dict:
    arg_keys = jax.random.split(jax.random.key(seed), 5)
    embeddings = draw_embeddings(jax.random.fold_in(arg_keys[4], 71), 0)
    cluster_ids = with_ends(jax.random.randint(arg_keys[1], (TILES, TILE_ROWS), 0, CLUSTERS), jax.random.fold_in(arg_keys[1], 1), 0, CLUSTERS - 1).astype(jnp.int32)
    owners_keys = jax.random.split(jax.random.fold_in(arg_keys[2], 1), TILES // TILES_DEV)
    owners_turns = jax.random.permutation(jax.random.fold_in(arg_keys[2], 3), TILES // TILES_DEV)
    owners = jax.vmap(lambda own, number: deal_out(jax.random.fold_in(arg_keys[2], 2), own, number, TILES_DEV, N_OWN, 1, CAPACITY, 2))(owners_keys, owners_turns).reshape((TILES, 1))
    pattern = with_ends((jax.random.randint(arg_keys[3], (N_GRP, N_GRP), 0, 4) < 3).astype(jnp.int32), jax.random.fold_in(arg_keys[3], 1), 0, 1)
    return dict(embeddings=embeddings, cluster_ids=cluster_ids, owners=owners, pattern=pattern)


def unit_rows(values):
    wide = values.astype(jnp.float32)
    return (wide * lax.rsqrt(lax.optimization_barrier(jnp.sum(wide * wide, axis=-1, keepdims=True)) + 1e-06)).astype(jnp.bfloat16)

def reference(embeddings, cluster_ids, owners, pattern):
    units = unit_rows(embeddings)
    panel_tiles = N_OWN * CAPACITY
    sub_tiles = 4 * CAPACITY
    blocks = panel_tiles // sub_tiles
    tile_rows = TILE_ROWS
    width = D
    zero = jnp.int32(0)
    target = owners[:, 0].astype(jnp.int32)
    tile_index = jnp.arange(TILES, dtype=jnp.int32)
    group_of = (tile_index // (TILES_DEV * N_OWN)).astype(jnp.int32)
    sort_key = (target * N_GRP + group_of).astype(jnp.int32)
    order = jnp.argsort(sort_key, stable=True).astype(jnp.int32)
    segments = jnp.arange(N_OWN * N_GRP, dtype=jnp.int32)
    counts = lax.optimization_barrier(jnp.sum((sort_key[None, :] == segments[:, None]).astype(jnp.int32), axis=1)).astype(jnp.int32)
    starts = (jnp.cumsum(counts) - counts).astype(jnp.int32)
    window = jnp.arange(panel_tiles, dtype=jnp.int32)

    def panel_of(segment):
        where_at = jnp.minimum(starts[segment] + window, TILES - 1).astype(jnp.int32)
        live = window < counts[segment]
        return jnp.where(live, order[where_at], -1).astype(jnp.int32)
    all_tiles = jax.vmap(panel_of)(segments).reshape(N_OWN, N_GRP, panel_tiles)
    count_grid = counts.reshape(N_OWN, N_GRP)
    row_offsets = jnp.arange(tile_rows, dtype=jnp.int32)

    def per_owner(inputs):
        tiles, owner_counts = inputs
        safe = jnp.maximum(tiles, 0)
        owner_units = units[safe]
        owner_ids = jnp.where((tiles >= 0)[:, :, None], cluster_ids[safe], -1).astype(jnp.int32)
        owner_rows = jnp.where((tiles >= 0)[:, :, None], safe[:, :, None] * tile_rows + row_offsets[None, None, :], -1).astype(jnp.int32)

        def query_block(q):
            q = q.astype(jnp.int32)
            g = (q // blocks).astype(jnp.int32)
            qb = (q % blocks).astype(jnp.int32)
            q_start = (qb * sub_tiles).astype(jnp.int32)
            q_units = lax.dynamic_slice(owner_units, (g, q_start, zero, zero), (1, sub_tiles, tile_rows, width)).reshape(sub_tiles * tile_rows, width)
            q_ids = lax.dynamic_slice(owner_ids, (g, q_start, zero), (1, sub_tiles, tile_rows)).reshape(-1)
            q_rows = lax.dynamic_slice(owner_rows, (g, q_start, zero), (1, sub_tiles, tile_rows)).reshape(-1)
            q_live = q_start < owner_counts[g]

            def key_step(k, best):
                k = jnp.asarray(k).astype(jnp.int32)
                h = (k // blocks).astype(jnp.int32)
                kb = (k % blocks).astype(jnp.int32)
                k_start = (kb * sub_tiles).astype(jnp.int32)
                live = q_live & (k_start < owner_counts[h]) & (pattern[g, h] > 0)

                def work(current):
                    k_units = lax.dynamic_slice(owner_units, (h, k_start, zero, zero), (1, sub_tiles, tile_rows, width)).reshape(sub_tiles * tile_rows, width)
                    k_ids = lax.dynamic_slice(owner_ids, (h, k_start, zero), (1, sub_tiles, tile_rows)).reshape(-1)
                    k_rows = lax.dynamic_slice(owner_rows, (h, k_start, zero), (1, sub_tiles, tile_rows)).reshape(-1)
                    scores = jnp.dot(q_units, k_units.T, preferred_element_type=jnp.float32)
                    match = (q_ids[:, None] == k_ids[None, :]) & (q_ids[:, None] >= 0) & (q_rows[:, None] != k_rows[None, :])
                    return jnp.maximum(current, lax.optimization_barrier(jnp.max(jnp.where(match, scores, jnp.float32(-1.0)), axis=1)))
                return lax.cond(live, work, lambda current: current, best)
            start_best = jnp.full((sub_tiles * tile_rows,), -1.0, dtype=jnp.float32)
            return lax.fori_loop(0, N_GRP * blocks, key_step, start_best)
        found = lax.map(query_block, jnp.arange(N_GRP * blocks, dtype=jnp.int32))
        return found.reshape(N_GRP, panel_tiles, tile_rows)
    results = lax.map(per_owner, (all_tiles, count_grid))
    dump = jnp.where(all_tiles >= 0, all_tiles, TILES).reshape(-1)
    output = jnp.zeros((TILES + 1, tile_rows), dtype=jnp.float32).at[dump].set(results.reshape(-1, tile_rows))
    return output[:TILES]
```

```python
import functools

import jax
import jax.numpy as jnp
from jax import lax
from jax.experimental import pallas as pl
from jax.experimental.pallas import tpu as pltpu
from jax.sharding import PartitionSpec as P


TILE = 32
GROUP = 8
ROWS = TILE * GROUP

TREE = (
    (1, (0, 0), (1, 0)),
    (1, (0, 0), (-1, 0)),
    (1, (0, 0), (0, 1)),
    (1, (0, 0), (0, -1)),
    (2, (0, 1), (1, 0)),
    (2, (0, -1), (-1, 0)),
    (2, (-1, 0), (0, 1)),
    (2, (1, 0), (0, -1)),
    (3, (1, 0), (1, 0)),
    (3, (-1, -1), (-1, 0)),
    (3, (0, 1), (0, 1)),
    (3, (1, -1), (0, -1)),
    (4, (1, 1), (1, 0)),
    (4, (-1, 1), (0, 1)),
    (4, (2, 3), (0, -1)),
)
SIDE = 4


def wrap(node):
    return (node[0] % SIDE, node[1] % SIDE)


def plane_pairs(dx, dy, flip):
    pairs = []
    for y in range(SIDE):
        for x in range(SIDE):
            for core in range(2):
                source = (y * SIDE + x) * 2 + core
                dest = (((y + dy) % SIDE) * SIDE + (x + dx) % SIDE) * 2 + (core ^ flip)
                pairs.append((source, dest))
    return pairs


def in_plane(value, dx, dy):
    return lax.ppermute(value, "grp", plane_pairs(dx, dy, 0))


def other_core(value):
    return lax.ppermute(value, "grp", plane_pairs(0, 0, 1))


def along(value, step, count):
    return lax.ppermute(value, "own", [(i, (i + step) % count) for i in range(count)])


def unit_rows(values):
    wide = values.astype(jnp.float32)
    return (wide * lax.rsqrt(jnp.sum(wide * wide, axis=-1, keepdims=True) + 1e-06)).astype(
        jnp.bfloat16
    )


def sort_plan(owner):
    count = owner.shape[0]
    index = jnp.arange(count, dtype=jnp.int32)
    less = owner[None, :] < owner[:, None]
    tie = (owner[None, :] == owner[:, None]) & (index[None, :] < index[:, None])
    place = jnp.sum((less | tie).astype(jnp.int32), axis=1)
    hot = (place[None, :] == index[:, None]).astype(jnp.float32)
    return place, hot


def compare_kernel(
    q_parts, k_parts, with_self, q_place, q_order, k_place, lo, hi, q_cls, k_cls, *refs
):
    n_q, n_k = len(q_parts), len(k_parts)
    q_refs, k_refs = refs[:n_q], refs[n_q : n_q + n_k]
    out_ref, q_pan, k_pan, acc, spread, sems = refs[n_q + n_k :]

    def gather(parts, sources, place, panel, sem):
        tile = 0
        for count, ref in zip(parts, sources):
            for j in range(count):
                to = pl.multiple_of(place[tile] * TILE, TILE)
                pltpu.make_async_copy(
                    ref.at[pl.ds(j * TILE, TILE)], panel.at[pl.ds(to, TILE)], sem
                ).start()
                tile += 1

    gather(q_parts, q_refs, q_place, q_pan, sems.at[0])
    gather(k_parts, k_refs, k_place, k_pan, sems.at[1])
    pltpu.make_async_copy(q_pan, q_pan, sems.at[0]).wait()
    pltpu.make_async_copy(k_pan, k_pan, sems.at[1]).wait()
    blocks = sum(q_parts) // GROUP

    def block_step(b, carry):
        row = jnp.broadcast_to(q_cls[b], (128, ROWS))
        q_col = jnp.transpose(row)
        if with_self:
            q_own = jnp.transpose(jnp.broadcast_to(q_cls[blocks + b], (128, ROWS)))
        acc[...] = jnp.full_like(acc, -1.0)

        def chunk_step(m, inner):
            keys = k_pan[pl.ds(pl.multiple_of(m * ROWS, ROWS), ROWS), :]
            queries = q_pan[pl.ds(pl.multiple_of(b * ROWS, ROWS), ROWS), :]
            scores = lax.dot_general(
                queries, keys, (((1,), (1,)), ((), ())), preferred_element_type=jnp.float32
            )
            best = acc[...]
            for h in range(ROWS // 128):
                lanes = slice(h * 128, (h + 1) * 128)
                match = q_col == k_cls[m][:, lanes]
                if with_self:
                    match = match & (q_own != k_cls[sum(k_parts) // GROUP + m][:, lanes])
                best = jnp.maximum(best, jnp.where(match, scores[:, lanes], -1.0))
            acc[...] = best
            return inner

        lax.fori_loop(lo[b], hi[b], chunk_step, 0)
        for j in range(GROUP):
            to = pl.multiple_of(q_order[b * GROUP + j] * TILE, TILE)
            spread[pl.ds(to, TILE), :] = acc[j * TILE : (j + 1) * TILE, :]
        return carry

    lax.fori_loop(0, blocks, block_step, 0)

    def out_step(s, carry):
        part = spread[pl.ds(pl.multiple_of(s * ROWS, ROWS), ROWS), :]
        out_ref[s] = jnp.max(jnp.transpose(part), axis=0, keepdims=True)
        return carry

    lax.fori_loop(0, blocks, out_step, 0)


def compare(q_arrays, k_arrays, q_class, k_class, q_own, k_own):
    q_parts = [a.shape[0] // TILE for a in q_arrays]
    k_parts = [a.shape[0] // TILE for a in k_arrays]
    n_q, n_k = sum(q_parts), sum(k_parts)
    width = q_arrays[0].shape[1]
    k_class, k_allowed = k_class
    q_owner, k_owner = q_class[:, 0] // 4, k_class[:, 0] // 4
    q_place, q_hot = sort_plan(q_owner)
    k_place, k_hot = sort_plan(k_owner)
    q_order = jnp.sum(q_hot * jnp.arange(n_q, dtype=jnp.float32)[None, :], axis=1).astype(jnp.int32)
    sorted_owner = jnp.sum(q_hot * q_owner[None, :].astype(jnp.float32), axis=1).reshape(-1, GROUP)
    first, last = sorted_owner[:, 0], sorted_owner[:, GROUP - 1]
    keys_owner = k_owner[None, :].astype(jnp.float32)
    lo = jnp.sum((keys_owner < first[:, None]).astype(jnp.int32), axis=1) // GROUP
    hi = (jnp.sum((keys_owner <= last[:, None]).astype(jnp.int32), axis=1) + GROUP - 1) // GROUP

    def in_order(hot, table):
        ordered = lax.dot_general(
            hot, table.astype(jnp.float32), (((1,), (0,)), ((), ())),
            precision=lax.Precision.HIGHEST,
        )
        return ordered.reshape(-1, 1, ROWS)

    q_cls = in_order(q_hot, q_class)
    k_cls = in_order(k_hot, k_allowed)
    with_self = q_own is not None
    if with_self:
        q_cls = jnp.concatenate([q_cls, in_order(q_hot, q_own)], axis=0)
        k_cls = jnp.concatenate([k_cls, in_order(k_hot, k_own)], axis=0)
    smem = pl.BlockSpec(memory_space=pltpu.SMEM)
    vmem = pl.BlockSpec(memory_space=pltpu.VMEM)
    anywhere = pl.BlockSpec(memory_space=pl.ANY)
    flops = 2 * n_q * n_k * TILE * TILE * width // 3
    return pl.pallas_call(
        functools.partial(compare_kernel, q_parts, k_parts, with_self),
        out_shape=jax.ShapeDtypeStruct((n_q // GROUP, 1, ROWS), jnp.float32),
        in_specs=[smem] * 5 + [vmem] * 2 + [anywhere] * (len(q_arrays) + len(k_arrays)),
        out_specs=vmem,
        scratch_shapes=[
            pltpu.VMEM((n_q * TILE, width), jnp.bfloat16),
            pltpu.VMEM((n_k * TILE, width), jnp.bfloat16),
            pltpu.VMEM((ROWS, 128), jnp.float32),
            pltpu.VMEM((n_q * TILE, 128), jnp.float32),
            pltpu.SemaphoreType.DMA((2,)),
        ],
        cost_estimate=pl.CostEstimate(
            flops=flops, bytes_accessed=(n_q + n_k) * TILE * width * 2, transcendentals=0
        ),
        name="compare",
    )(q_place, q_order, k_place, lo, hi, q_cls, k_cls, *q_arrays, *k_arrays)


def on_device(embeddings, cluster_ids, owners, pattern):
    n_own = lax.axis_size("own")
    n_grp = lax.axis_size("grp")
    tiles_here, tile_rows, width = embeddings.shape
    group = lax.axis_index("grp")
    depth = lax.axis_index("own")
    units = unit_rows(embeddings).reshape(tiles_here * tile_rows, width)
    classes = owners * 4 + cluster_ids

    line_class = lax.all_to_all(
        jnp.broadcast_to(classes[None], (n_own,) + classes.shape), "own", 0, 0, tiled=True
    ).reshape(n_own, tiles_here, tile_rows)
    plane_class = lax.all_to_all(
        jnp.broadcast_to(classes[None], (n_grp,) + classes.shape), "grp", 0, 0, tiled=True
    ).reshape(n_grp, tiles_here, tile_rows)

    up, down = [units], [units]
    line = [units]
    steps = [0]
    for hop in range(1, n_own // 2):
        up.append(along(up[-1], 1, n_own))
        down.append(along(down[-1], -1, n_own))
        line += [up[-1], down[-1]]
        steps += [hop, -hop]
    half = units.shape[0] // 2
    far_low = along(up[-1][:half], 1, n_own)
    far_high = along(down[-1][half:], -1, n_own)
    line += [far_low, far_high]
    steps.append(n_own // 2)

    held = {(0, 0): units}
    swapped = {(0, 0): other_core(units)}
    nodes = {1: [(0, 0)], 2: []}
    for turn, source, (dx, dy) in TREE:
        node = wrap((source[0] + dx, source[1] + dy))
        held[node] = in_plane(held[wrap(source)], dx, dy)
        swapped[node] = other_core(held[node])
        nodes[1 if turn < 4 else 2].append(node)

    core = group % 2
    chip_x, chip_y = (group // 2) % SIDE, group // (2 * SIDE)
    allowed_row = jnp.sum(
        pattern * (jnp.arange(n_grp, dtype=jnp.int32)[:, None] == group).astype(jnp.int32), axis=0
    )
    line_from = jnp.stack([(depth - s) % n_own for s in steps])
    q_class = jnp.take(line_class, line_from, axis=0).reshape(-1, tile_rows)
    slot_allowed = jnp.broadcast_to(
        allowed_row[:, None, None] > 0, plane_class.shape
    )
    plane_allowed = jnp.where(slot_allowed, plane_class, -1)
    row_names = jnp.arange(tiles_here * tile_rows, dtype=jnp.int32).reshape(tiles_here, tile_rows)

    results = []
    for call in (1, 2):
        k_arrays, k_from = [], []
        for dx, dy in nodes[call]:
            base = (((chip_y - dy) % SIDE) * SIDE + (chip_x - dx) % SIDE) * 2
            k_arrays += [held[(dx, dy)], swapped[(dx, dy)]]
            k_from += [base + core, base + 1 - core]
        k_from = jnp.stack(k_from)
        k_class = (
            jnp.take(plane_class, k_from, axis=0).reshape(-1, tile_rows),
            jnp.take(plane_allowed, k_from, axis=0).reshape(-1, tile_rows),
        )
        q_own = k_own = None
        if call == 1:
            q_own = jnp.full(q_class.shape, -1, jnp.int32).at[:tiles_here].set(row_names)
            k_own = jnp.full(k_class[0].shape, -2, jnp.int32).at[:tiles_here].set(row_names)
        results.append(compare(line, k_arrays, q_class, k_class, q_own, k_own))
    best = jnp.maximum(results[0], results[1]).reshape(n_own, -1)

    slot_of = [0] * n_own
    for place, s in enumerate(steps):
        slot_of[s % n_own] = place
    slot_of = jnp.array(slot_of, jnp.int32)
    send = best[slot_of[(depth - jnp.arange(n_own, dtype=jnp.int32)) % n_own]]
    returned = lax.all_to_all(send, "own", split_axis=0, concat_axis=0, tiled=True)
    return jnp.max(returned, axis=0).reshape(tiles_here, tile_rows)


def solution(mesh):
    placed = (P(("grp", "own"), None, None), P(("grp", "own"), None), P(("grp", "own"), None), P())
    return jax.shard_map(
        on_device, mesh=mesh, in_specs=placed, out_specs=P(("grp", "own"), None), check_vma=False
    )
```

```python
import functools

import jax
import jax.numpy as jnp
from jax import lax
from jax.experimental import pallas as pl
from jax.experimental.pallas import tpu as pltpu
from jax.sharding import PartitionSpec as P


TILE = 32
GROUP = 8
ROWS = TILE * GROUP
CHUNK = 2 * ROWS

TREE = (
    (1, (0, 0), (1, 0)),
    (1, (0, 0), (-1, 0)),
    (1, (0, 0), (0, 1)),
    (1, (0, 0), (0, -1)),
    (2, (0, 1), (1, 0)),
    (2, (0, -1), (-1, 0)),
    (2, (-1, 0), (0, 1)),
    (2, (1, 0), (0, -1)),
    (3, (1, 0), (1, 0)),
    (3, (-1, -1), (-1, 0)),
    (3, (0, 1), (0, 1)),
    (3, (1, -1), (0, -1)),
    (4, (1, 1), (1, 0)),
    (4, (-1, 1), (0, 1)),
    (4, (2, 3), (0, -1)),
)
SIDE = 4


def wrap(node):
    return (node[0] % SIDE, node[1] % SIDE)


def plane_pairs(dx, dy, flip):
    pairs = []
    for y in range(SIDE):
        for x in range(SIDE):
            for core in range(2):
                source = (y * SIDE + x) * 2 + core
                dest = (((y + dy) % SIDE) * SIDE + (x + dx) % SIDE) * 2 + (core ^ flip)
                pairs.append((source, dest))
    return pairs


def in_plane(value, dx, dy):
    return lax.ppermute(value, "grp", plane_pairs(dx, dy, 0))


def other_core(value):
    return lax.ppermute(value, "grp", plane_pairs(0, 0, 1))


def along(value, step, count):
    return lax.ppermute(value, "own", [(i, (i + step) % count) for i in range(count)])


def unit_rows(values):
    wide = values.astype(jnp.float32)
    return (wide * lax.rsqrt(jnp.sum(wide * wide, axis=-1, keepdims=True) + 1e-06)).astype(
        jnp.bfloat16
    )


def sort_plan(owner):
    count = owner.shape[0]
    index = jnp.arange(count, dtype=jnp.int32)
    less = owner[None, :] < owner[:, None]
    tie = (owner[None, :] == owner[:, None]) & (index[None, :] < index[:, None])
    place = jnp.sum((less | tie).astype(jnp.int32), axis=1)
    hot = (place[None, :] == index[:, None]).astype(jnp.float32)
    return place, hot


def compare_kernel(
    q_parts, k_parts, with_self, q_place, q_order, k_place, lo, hi, q_cls, k_cls, *refs
):
    n_q, n_k = len(q_parts), len(k_parts)
    q_refs, k_refs = refs[:n_q], refs[n_q : n_q + n_k]
    out_ref, q_pan, k_pan, acc, spread, sems = refs[n_q + n_k :]

    def gather(parts, sources, place, panel, sem):
        tile = 0
        for count, ref in zip(parts, sources):
            for j in range(count):
                to = pl.multiple_of(place[tile] * TILE, TILE)
                pltpu.make_async_copy(
                    ref.at[pl.ds(j * TILE, TILE)], panel.at[pl.ds(to, TILE)], sem
                ).start()
                tile += 1

    gather(q_parts, q_refs, q_place, q_pan, sems.at[0])
    gather(k_parts, k_refs, k_place, k_pan, sems.at[1])
    pltpu.make_async_copy(q_pan, q_pan, sems.at[0]).wait()
    pltpu.make_async_copy(k_pan, k_pan, sems.at[1]).wait()
    blocks = sum(q_parts) // GROUP

    def block_step(b, carry):
        row = jnp.broadcast_to(q_cls[b], (128, ROWS))
        q_col = jnp.transpose(row)
        if with_self:
            q_own = jnp.transpose(jnp.broadcast_to(q_cls[blocks + b], (128, ROWS)))
        acc[...] = jnp.full_like(acc, -1.0)

        def chunk_step(m, inner):
            keys = k_pan[pl.ds(pl.multiple_of(m * CHUNK, CHUNK), CHUNK), :]
            queries = q_pan[pl.ds(pl.multiple_of(b * ROWS, ROWS), ROWS), :]
            scores = lax.dot_general(
                queries, keys, (((1,), (1,)), ((), ())), preferred_element_type=jnp.float32
            )
            best = acc[...]
            for h in range(CHUNK // 128):
                lanes = slice(h * 128, (h + 1) * 128)
                match = q_col == k_cls[m][:, lanes]
                if with_self:
                    match = match & (q_own != k_cls[sum(k_parts) * TILE // CHUNK + m][:, lanes])
                best = jnp.maximum(best, jnp.where(match, scores[:, lanes], -1.0))
            acc[...] = best
            return inner

        lax.fori_loop(lo[b], hi[b], chunk_step, 0)
        for j in range(GROUP):
            to = pl.multiple_of(q_order[b * GROUP + j] * TILE, TILE)
            spread[pl.ds(to, TILE), :] = acc[j * TILE : (j + 1) * TILE, :]
        return carry

    lax.fori_loop(0, blocks, block_step, 0)

    def out_step(s, carry):
        part = spread[pl.ds(pl.multiple_of(s * ROWS, ROWS), ROWS), :]
        out_ref[s] = jnp.max(jnp.transpose(part), axis=0, keepdims=True)
        return carry

    lax.fori_loop(0, blocks, out_step, 0)


def compare(q_arrays, k_arrays, q_class, k_class, q_own, k_own):
    q_parts = [a.shape[0] // TILE for a in q_arrays]
    k_parts = [a.shape[0] // TILE for a in k_arrays]
    n_q, n_k = sum(q_parts), sum(k_parts)
    width = q_arrays[0].shape[1]
    k_class, k_allowed = k_class
    q_owner, k_owner = q_class[:, 0] // 4, k_class[:, 0] // 4
    q_place, q_hot = sort_plan(q_owner)
    k_place, k_hot = sort_plan(k_owner)
    q_order = jnp.sum(q_hot * jnp.arange(n_q, dtype=jnp.float32)[None, :], axis=1).astype(jnp.int32)
    sorted_owner = jnp.sum(q_hot * q_owner[None, :].astype(jnp.float32), axis=1).reshape(-1, GROUP)
    first, last = sorted_owner[:, 0], sorted_owner[:, GROUP - 1]
    keys_owner = k_owner[None, :].astype(jnp.float32)
    per = CHUNK // TILE
    lo = jnp.sum((keys_owner < first[:, None]).astype(jnp.int32), axis=1) // per
    hi = (jnp.sum((keys_owner <= last[:, None]).astype(jnp.int32), axis=1) + per - 1) // per

    def in_order(hot, table, wide):
        ordered = lax.dot_general(
            hot, table.astype(jnp.float32), (((1,), (0,)), ((), ())),
            precision=lax.Precision.HIGHEST,
        )
        return ordered.reshape(-1, 1, wide)

    q_cls = in_order(q_hot, q_class, ROWS)
    k_cls = in_order(k_hot, k_allowed, CHUNK)
    with_self = q_own is not None
    if with_self:
        q_cls = jnp.concatenate([q_cls, in_order(q_hot, q_own, ROWS)], axis=0)
        k_cls = jnp.concatenate([k_cls, in_order(k_hot, k_own, CHUNK)], axis=0)
    smem = pl.BlockSpec(memory_space=pltpu.SMEM)
    vmem = pl.BlockSpec(memory_space=pltpu.VMEM)
    anywhere = pl.BlockSpec(memory_space=pl.ANY)
    flops = 2 * n_q * n_k * TILE * TILE * width // 3
    return pl.pallas_call(
        functools.partial(compare_kernel, q_parts, k_parts, with_self),
        out_shape=jax.ShapeDtypeStruct((n_q // GROUP, 1, ROWS), jnp.float32),
        in_specs=[smem] * 5 + [vmem] * 2 + [anywhere] * (len(q_arrays) + len(k_arrays)),
        out_specs=vmem,
        scratch_shapes=[
            pltpu.VMEM((n_q * TILE, width), jnp.bfloat16),
            pltpu.VMEM((n_k * TILE, width), jnp.bfloat16),
            pltpu.VMEM((ROWS, 128), jnp.float32),
            pltpu.VMEM((n_q * TILE, 128), jnp.float32),
            pltpu.SemaphoreType.DMA((2,)),
        ],
        cost_estimate=pl.CostEstimate(
            flops=flops, bytes_accessed=(n_q + n_k) * TILE * width * 2, transcendentals=0
        ),
        name="compare",
    )(q_place, q_order, k_place, lo, hi, q_cls, k_cls, *q_arrays, *k_arrays)


def search(embeddings, cluster_ids, owners, pattern):
    n_own = lax.axis_size("own")
    n_grp = lax.axis_size("grp")
    tiles_here, tile_rows, width = embeddings.shape
    group = lax.axis_index("grp")
    depth = lax.axis_index("own")
    units = unit_rows(embeddings).reshape(tiles_here * tile_rows, width)
    classes = owners * 4 + cluster_ids

    line_class = lax.all_to_all(
        jnp.broadcast_to(classes[None], (n_own,) + classes.shape), "own", 0, 0, tiled=True
    ).reshape(n_own, tiles_here, tile_rows)
    plane_class = lax.all_to_all(
        jnp.broadcast_to(classes[None], (n_grp,) + classes.shape), "grp", 0, 0, tiled=True
    ).reshape(n_grp, tiles_here, tile_rows)

    up, down = [units], [units]
    line = [units]
    steps = [0]
    for hop in range(1, n_own // 2):
        up.append(along(up[-1], 1, n_own))
        down.append(along(down[-1], -1, n_own))
        line += [up[-1], down[-1]]
        steps += [hop, -hop]
    half = units.shape[0] // 2
    far_low = along(up[-1][:half], 1, n_own)
    far_high = along(down[-1][half:], -1, n_own)
    line += [far_low, far_high]
    steps.append(n_own // 2)

    held = {(0, 0): units}
    swapped = {(0, 0): other_core(units)}
    nodes = {1: [(0, 0)], 2: []}
    for turn, source, (dx, dy) in TREE:
        node = wrap((source[0] + dx, source[1] + dy))
        held[node] = in_plane(held[wrap(source)], dx, dy)
        swapped[node] = other_core(held[node])
        nodes[1 if turn < 4 else 2].append(node)

    core = group % 2
    chip_x, chip_y = (group // 2) % SIDE, group // (2 * SIDE)
    allowed_row = jnp.sum(
        pattern * (jnp.arange(n_grp, dtype=jnp.int32)[:, None] == group).astype(jnp.int32), axis=0
    )
    line_from = jnp.stack([(depth - s) % n_own for s in steps])
    q_class = jnp.take(line_class, line_from, axis=0).reshape(-1, tile_rows)
    slot_allowed = jnp.broadcast_to(
        allowed_row[:, None, None] > 0, plane_class.shape
    )
    plane_allowed = jnp.where(slot_allowed, plane_class, -1)
    row_names = jnp.arange(tiles_here * tile_rows, dtype=jnp.int32).reshape(tiles_here, tile_rows)

    results = []
    for call in (1, 2):
        k_arrays, k_from = [], []
        for dx, dy in nodes[call]:
            base = (((chip_y - dy) % SIDE) * SIDE + (chip_x - dx) % SIDE) * 2
            k_arrays += [held[(dx, dy)], swapped[(dx, dy)]]
            k_from += [base + core, base + 1 - core]
        k_from = jnp.stack(k_from)
        k_class = (
            jnp.take(plane_class, k_from, axis=0).reshape(-1, tile_rows),
            jnp.take(plane_allowed, k_from, axis=0).reshape(-1, tile_rows),
        )
        q_own = k_own = None
        if call == 1:
            q_own = jnp.full(q_class.shape, -1, jnp.int32).at[:tiles_here].set(row_names)
            k_own = jnp.full(k_class[0].shape, -2, jnp.int32).at[:tiles_here].set(row_names)
        results.append(compare(line, k_arrays, q_class, k_class, q_own, k_own))
    best = jnp.maximum(results[0], results[1]).reshape(n_own, -1)

    slot_of = [0] * n_own
    for place, s in enumerate(steps):
        slot_of[s % n_own] = place
    slot_of = jnp.array(slot_of, jnp.int32)
    send = best[slot_of[(depth - jnp.arange(n_own, dtype=jnp.int32)) % n_own]]
    returned = lax.all_to_all(send, "own", split_axis=0, concat_axis=0, tiled=True)
    return jnp.max(returned, axis=0).reshape(tiles_here, tile_rows)


def solution(mesh):
    placed = (P(("grp", "own"), None, None), P(("grp", "own"), None), P(("grp", "own"), None), P())
    return jax.shard_map(
        search, mesh=mesh, in_specs=placed, out_specs=P(("grp", "own"), None), check_vma=False
    )
```

```python
import functools

import jax
import jax.numpy as jnp
from jax import lax
from jax.experimental import pallas as pl
from jax.experimental.pallas import tpu as pltpu
from jax.sharding import PartitionSpec as P


TILE = 32
GROUP = 8
ROWS = TILE * GROUP
CHUNK = 2 * ROWS

TREE = (
    (1, (0, 0), (1, 0)),
    (1, (0, 0), (-1, 0)),
    (1, (0, 0), (0, 1)),
    (1, (0, 0), (0, -1)),
    (2, (0, 1), (1, 0)),
    (2, (0, -1), (-1, 0)),
    (2, (-1, 0), (0, 1)),
    (2, (1, 0), (0, -1)),
    (3, (1, 0), (1, 0)),
    (3, (-1, -1), (-1, 0)),
    (3, (0, 1), (0, 1)),
    (3, (1, -1), (0, -1)),
    (4, (1, 1), (1, 0)),
    (4, (-1, 1), (0, 1)),
    (4, (2, 3), (0, -1)),
)
SIDE = 4
OWNERS = 8
CLUSTERS = 4


def wrap(node):
    return (node[0] % SIDE, node[1] % SIDE)


def plane_pairs(dx, dy, flip):
    pairs = []
    for y in range(SIDE):
        for x in range(SIDE):
            for core in range(2):
                source = (y * SIDE + x) * 2 + core
                dest = (((y + dy) % SIDE) * SIDE + (x + dx) % SIDE) * 2 + (core ^ flip)
                pairs.append((source, dest))
    return pairs


def in_plane(value, dx, dy):
    return lax.ppermute(value, "grp", plane_pairs(dx, dy, 0))


def other_core(value):
    return lax.ppermute(value, "grp", plane_pairs(0, 0, 1))


def along(value, step, count):
    return lax.ppermute(value, "own", [(i, (i + step) % count) for i in range(count)])


def unit_rows(values):
    wide = values.astype(jnp.float32)
    return (wide * lax.rsqrt(jnp.sum(wide * wide, axis=-1, keepdims=True) + 1e-06)).astype(
        jnp.bfloat16
    )


def compare_kernel(queries, keys, with_self, with_prev, where_ref, pattern_ref, *refs):
    n_ops = max([h for _, h, _ in queries] + [k[0] for k in keys]) + 1
    arrays = refs[:n_ops]
    refs = refs[n_ops:]
    if with_prev:
        prev_ref, refs = refs[0], refs[1:]
    out_ref, q_pan, k_pan, q_col, k_col, acc, spread, meta, own_vec = refs[:9]
    own_s, q_base, k_base, q_next, k_next, q_order, q_own_s, k_place, q_place, sems = refs[9:19]
    if with_self:
        q_self, k_self = refs[19:21]
    n_q, n_k = len(queries), len(keys)
    k_tiles = n_k * GROUP
    per = CHUNK // TILE
    group, depth = where_ref[0], where_ref[1]
    chip_y, chip_x, core = group // (2 * SIDE), (group // 2) % SIDE, group % 2

    for i in range(n_q + n_k):
        if i < n_q:
            low, high, _ = queries[i]
            row = ROWS if low == high else ROWS // 2
        else:
            high, row = keys[i - n_q][0], ROWS
        pltpu.make_async_copy(
            arrays[high].at[pl.ds(row, 8), pl.ds(0, ROWS)], meta.at[i], sems.at[0]
        ).start()
    pltpu.make_async_copy(meta, meta, sems.at[0]).wait()
    for i in range(n_q + n_k):
        own_vec[i : i + 1, :] = meta[i].astype(jnp.float32)[1:2, :].astype(jnp.int32)
    to_scalar = pltpu.make_async_copy(own_vec, own_s, sems.at[0])
    to_scalar.start()
    to_scalar.wait()

    for o in range(OWNERS + 1):
        q_next[o] = 0
        k_next[o] = 0

    def count(i, table):
        for j in range(GROUP):
            o = own_s[i, j * TILE]
            table[o] = table[o] + 1

    def count_q(i, carry):
        count(i, q_next)
        return carry

    def count_k(i, carry):
        count(i, k_next)
        return carry

    lax.fori_loop(0, n_q, count_q, 0)
    lax.fori_loop(n_q, n_q + n_k, count_k, 0)
    for base, table in ((q_base, q_next), (k_base, k_next)):
        total = jnp.int32(0)
        for o in range(OWNERS + 1):
            here = table[o]
            base[o] = total
            table[o] = total
            total = total + here

    for i in range(n_q):
        low, high, _ = queries[i]
        for first, ref, shift in ((0, low, 0), (GROUP // 2, high, 0 if low == high else GROUP // 2)):

            def put_q(j, carry, i=i, ref=ref, shift=shift):
                o = own_s[i, j * TILE]
                to = q_next[o]
                q_next[o] = to + 1
                q_order[to] = i * GROUP + j
                q_own_s[to] = o
                q_place[i * GROUP + j] = to
                pltpu.make_async_copy(
                    arrays[ref].at[pl.ds(pl.multiple_of((j - shift) * TILE, TILE), TILE)],
                    q_pan.at[pl.ds(pl.multiple_of(to * TILE, TILE), TILE)],
                    sems.at[1],
                ).start()
                return carry

            lax.fori_loop(first, first + GROUP // 2, put_q, 0, unroll=True)
    for i in range(n_k):
        src = arrays[keys[i][0]]

        def put_k(j, carry, i=i, src=src):
            o = own_s[n_q + i, j * TILE]
            to = k_next[o]
            k_next[o] = to + 1
            k_place[i * GROUP + j] = to
            pltpu.make_async_copy(
                src.at[pl.ds(pl.multiple_of(j * TILE, TILE), TILE), pl.ds(0, src.shape[1])],
                k_pan.at[pl.ds(pl.multiple_of(to * TILE, TILE), TILE)],
                sems.at[2],
            ).start()
            return carry

        lax.fori_loop(0, GROUP, put_k, 0, unroll=True)

    def column(row):
        return jnp.transpose(jnp.broadcast_to(row, (128, ROWS)))

    def spread_column(col, place, i, panel):
        for j in range(GROUP):
            to = pl.multiple_of(place[i * GROUP + j] * TILE, TILE)
            panel[pl.ds(to, TILE), :] = col[j * TILE : (j + 1) * TILE, :]

    def label(i):
        info = meta[i].astype(jnp.float32)
        return info[1:2, :] * CLUSTERS + info[0:1, :]

    for i in range(n_q):
        spread_column(column(label(i)), q_place, i, q_col)
    for i in range(n_k):
        _, dx, dy, flip = keys[i]
        source = (((chip_y - dy) % SIDE) * SIDE + (chip_x - dx) % SIDE) * 2 + (core + flip) % 2
        allowed = pattern_ref[group, source] > 0
        spread_column(column(jnp.where(allowed, label(n_q + i), -1.0)), k_place, i, k_col)
    if with_self:
        q_self[...] = jnp.full_like(q_self, -1.0)
        k_self[...] = jnp.full_like(k_self, -2.0)
        names = lax.broadcasted_iota(jnp.int32, (ROWS, 128), 0).astype(jnp.float32)
        spread_column(names, q_place, 0, q_self)
        spread_column(names, k_place, 0, k_self)
    pltpu.make_async_copy(q_pan, q_pan, sems.at[1]).wait()
    pltpu.make_async_copy(k_pan, k_pan, sems.at[2]).wait()

    def block_step(b, carry):
        rows = pl.ds(pl.multiple_of(b * ROWS, ROWS), ROWS)
        q_row = jnp.transpose(q_col[rows, :])[0:1, :]
        if with_self:
            q_name = jnp.transpose(q_self[rows, :])[0:1, :]
        acc[...] = jnp.full_like(acc, -1.0)
        lo = k_base[q_own_s[b * GROUP]]
        hi = k_base[q_own_s[b * GROUP + GROUP - 1] + 1]

        def chunk_step(m, inner):
            at = pl.multiple_of(jnp.minimum(lo + m * per, k_tiles - per) * TILE, TILE)
            span = pl.ds(at, CHUNK)
            scores = lax.dot_general(
                k_pan[span, :], q_pan[rows, :], (((1,), (1,)), ((), ())),
                preferred_element_type=jnp.float32,
            )
            col = k_col[span, :]
            if with_self:
                name = k_self[span, :]
            for h in range(ROWS // 128):
                lanes = slice(h * 128, (h + 1) * 128)
                match = col == q_row[:, lanes]
                if with_self:
                    match = match & (name != q_name[:, lanes])
                found = jnp.where(match, scores[:, lanes], -1.0)
                found = jnp.max(found.reshape(CHUNK // 8, 8, 128), axis=0)
                acc[:, lanes] = jnp.maximum(acc[:, lanes], found)
            return inner

        lax.fori_loop(0, (hi - lo + per - 1) // per, chunk_step, 0)
        done = column(jnp.max(acc[...], axis=0, keepdims=True))
        for j in range(GROUP):
            to = pl.multiple_of(q_order[b * GROUP + j] * TILE, TILE)
            spread[pl.ds(to, TILE), :] = done[j * TILE : (j + 1) * TILE, :]
        return carry

    lax.fori_loop(0, n_q, block_step, 0)
    for s in range(n_q):
        row = jnp.transpose(spread[s * ROWS : (s + 1) * ROWS, :])[0:1, :]
        to = (depth - queries[s][2] + 2 * n_q) % n_q
        if with_prev:
            row = jnp.maximum(row, prev_ref[to])
        out_ref[to] = row


def compare(where, pattern, arrays, queries, keys, with_self, prev=None):
    n_q, n_k = len(queries), len(keys)
    width = arrays[0].shape[1]
    smem = pl.BlockSpec(memory_space=pltpu.SMEM)
    vmem = pl.BlockSpec(memory_space=pltpu.VMEM)
    anywhere = pl.BlockSpec(memory_space=pl.ANY)
    slots = -(-(n_q + n_k) // 8) * 8
    scratch = [
        pltpu.VMEM((n_q * ROWS, width), jnp.bfloat16),
        pltpu.VMEM((n_k * ROWS, width), jnp.bfloat16),
        pltpu.VMEM((n_q * ROWS, 128), jnp.float32),
        pltpu.VMEM((n_k * ROWS, 128), jnp.float32),
        pltpu.VMEM((8, ROWS), jnp.float32),
        pltpu.VMEM((n_q * ROWS, 128), jnp.float32),
        pltpu.VMEM((n_q + n_k, 8, ROWS), jnp.bfloat16),
        pltpu.VMEM((slots, ROWS), jnp.int32),
        pltpu.SMEM((slots, ROWS), jnp.int32),
        pltpu.SMEM((OWNERS + 1,), jnp.int32),
        pltpu.SMEM((OWNERS + 1,), jnp.int32),
        pltpu.SMEM((OWNERS + 1,), jnp.int32),
        pltpu.SMEM((OWNERS + 1,), jnp.int32),
        pltpu.SMEM((n_q * GROUP,), jnp.int32),
        pltpu.SMEM((n_q * GROUP,), jnp.int32),
        pltpu.SMEM((n_k * GROUP,), jnp.int32),
        pltpu.SMEM((n_q * GROUP,), jnp.int32),
        pltpu.SemaphoreType.DMA((3,)),
    ]
    if with_self:
        scratch += [
            pltpu.VMEM((n_q * ROWS, 128), jnp.float32),
            pltpu.VMEM((n_k * ROWS, 128), jnp.float32),
        ]
    extra = () if prev is None else (prev,)
    return pl.pallas_call(
        functools.partial(compare_kernel, queries, keys, with_self, prev is not None),
        out_shape=jax.ShapeDtypeStruct((n_q, 1, ROWS), jnp.float32),
        in_specs=[smem] * 2 + [anywhere] * len(arrays) + [vmem] * len(extra),
        out_specs=vmem,
        scratch_shapes=scratch,
        cost_estimate=pl.CostEstimate(
            flops=2 * n_q * n_k * ROWS * ROWS * width // 3,
            bytes_accessed=(n_q + n_k) * ROWS * width * 2,
            transcendentals=0,
        ),
        name="compare",
    )(where, pattern, *arrays, *extra)


def search(embeddings, cluster_ids, owners, pattern):
    n_own = lax.axis_size("own")
    tiles_here, tile_rows, width = embeddings.shape
    where = jnp.stack([lax.axis_index("grp"), lax.axis_index("own")]).astype(jnp.int32)

    labels = jnp.stack([cluster_ids, jnp.broadcast_to(owners, cluster_ids.shape)])
    labels = labels.reshape(2, ROWS).astype(jnp.bfloat16)
    labels = jnp.pad(labels, ((0, 6), (0, width - ROWS)))
    shard = jnp.concatenate([unit_rows(embeddings).reshape(ROWS, width), labels], axis=0)

    up, down = [shard], [shard]
    line = [shard]
    queries = [(0, 0, 0)]
    for hop in range(1, n_own // 2):
        up.append(along(up[-1], 1, n_own))
        down.append(along(down[-1], -1, n_own))
        queries += [(len(line), len(line), hop), (len(line) + 1, len(line) + 1, -hop)]
        line += [up[-1], down[-1]]
    far_low = along(up[-1][: ROWS // 2], 1, n_own)
    far_high = along(down[-1][ROWS // 2 :], -1, n_own)
    queries.append((len(line), len(line) + 1, n_own // 2))
    line += [far_low, far_high]

    held = {(0, 0): shard}
    swapped = {(0, 0): other_core(shard)}
    nodes = {1: [(0, 0)], 2: []}
    for turn, source, (dx, dy) in TREE:
        node = wrap((source[0] + dx, source[1] + dy))
        held[node] = in_plane(held[wrap(source)], dx, dy)
        swapped[node] = other_core(held[node])
        nodes[1 if turn < 4 else 2].append(node)

    best = None
    for call in (1, 2):
        arrays, keys = list(line), []
        for dx, dy in nodes[call]:
            for flip, table in enumerate((held, swapped)):
                if (dx, dy, flip) == (0, 0, 0):
                    keys.append((0, 0, 0, 0))
                else:
                    keys.append((len(arrays), dx, dy, flip))
                    arrays.append(table[(dx, dy)])
        best = compare(where, pattern, arrays, queries, keys, call == 1, best)

    returned = lax.all_to_all(best, "own", split_axis=0, concat_axis=0, tiled=True)
    return jnp.max(returned, axis=0).reshape(tiles_here, tile_rows)


def solution(mesh):
    placed = (P(("grp", "own"), None, None), P(("grp", "own"), None), P(("grp", "own"), None), P())
    return jax.shard_map(
        search, mesh=mesh, in_specs=placed, out_specs=P(("grp", "own"), None), check_vma=False
    )
```

```python
import functools

import jax
import jax.numpy as jnp
from jax import lax
from jax.experimental import pallas as pl
from jax.experimental.pallas import tpu as pltpu
from jax.sharding import PartitionSpec as P


TILE = 32
GROUP = 8
ROWS = TILE * GROUP
CHUNKS = (4 * ROWS, 5 * ROWS)

TREE = (
    ((0, 0), (1, 0)),
    ((0, 0), (-1, 0)),
    ((0, 0), (0, 1)),
    ((0, 0), (0, -1)),
    ((0, 1), (1, 0)),
    ((0, -1), (-1, 0)),
    ((-1, 0), (0, 1)),
    ((1, 0), (0, -1)),
    ((1, 0), (1, 0)),
    ((-1, -1), (-1, 0)),
    ((0, 1), (0, 1)),
    ((1, -1), (0, -1)),
    ((1, 1), (1, 0)),
    ((-1, 1), (0, 1)),
    ((2, 3), (0, -1)),
)
SIDE = 4
OWNERS = 8
CLUSTERS = 4


def wrap(node):
    return (node[0] % SIDE, node[1] % SIDE)


def plane_pairs(dx, dy, flip):
    pairs = []
    for y in range(SIDE):
        for x in range(SIDE):
            for core in range(2):
                source = (y * SIDE + x) * 2 + core
                dest = (((y + dy) % SIDE) * SIDE + (x + dx) % SIDE) * 2 + (core ^ flip)
                pairs.append((source, dest))
    return pairs


def in_plane(value, dx, dy):
    return lax.ppermute(value, "grp", plane_pairs(dx, dy, 0))


def other_core(value):
    return lax.ppermute(value, "grp", plane_pairs(0, 0, 1))


def along(value, step, count):
    return lax.ppermute(value, "own", [(i, (i + step) % count) for i in range(count)])


def unit_rows(values):
    wide = values.astype(jnp.float32)
    return (wide * lax.rsqrt(jnp.sum(wide * wide, axis=-1, keepdims=True) + 1e-06)).astype(
        jnp.bfloat16
    )


def compare_kernel(queries, keys, where_ref, pattern_ref, *refs):
    n_ops = max([h for _, h, _ in queries] + [k[0] for k in keys]) + 1
    arrays = refs[:n_ops]
    out_ref, q_raw, k_raw, q_col, k_col, acc, spread, meta, own_vec = refs[n_ops : n_ops + 9]
    own_s, k_base, q_next, k_next, q_order, q_own_s, k_order, sems = refs[n_ops + 9 : n_ops + 17]
    q_rows, q_names, found_rows = refs[n_ops + 17 :]
    n_q, n_k = len(queries), len(keys)
    k_tiles, blocks = n_k * GROUP, n_q + OWNERS
    small, large = (chunk // TILE for chunk in CHUNKS)
    half = ROWS // 2
    group, depth = where_ref[0], where_ref[1]
    chip_y, chip_x, core = group // (2 * SIDE), (group // 2) % SIDE, group % 2

    for i in range(n_q + n_k):
        if i < n_q:
            low, high, _ = queries[i]
            row = ROWS if low == high else half
        else:
            high, row = keys[i - n_q][0], ROWS
        pltpu.make_async_copy(
            arrays[high].at[pl.ds(row, 8), pl.ds(0, ROWS)], meta.at[i], sems.at[0]
        ).start()
    for i in range(n_q):
        low, high, _ = queries[i]
        if low == high:
            parts = [(low, i * ROWS, ROWS)]
        else:
            parts = [(low, i * ROWS, half), (high, i * ROWS + half, half)]
        for ref, to, rows in parts:
            pltpu.make_async_copy(
                arrays[ref].at[pl.ds(0, rows)], q_raw.at[pl.ds(to, rows)], sems.at[1]
            ).start()
    for i in range(n_k):
        pltpu.make_async_copy(
            arrays[keys[i][0]].at[pl.ds(0, ROWS)], k_raw.at[pl.ds(i * ROWS, ROWS)], sems.at[2]
        ).start()
    pltpu.make_async_copy(meta, meta, sems.at[0]).wait()
    for i in range(n_q + n_k):
        own_vec[i : i + 1, :] = meta[i].astype(jnp.float32)[1:2, :].astype(jnp.int32)
    to_scalar = pltpu.make_async_copy(own_vec, own_s, sems.at[0])
    to_scalar.start()

    def column(row):
        return jnp.transpose(jnp.broadcast_to(row, (128, ROWS)))

    def label(i):
        info = meta[i].astype(jnp.float32)
        return info[1:2, :] * CLUSTERS + info[0:1, :]

    for i in range(n_q):
        q_col[i * ROWS : (i + 1) * ROWS, :] = column(label(i))
    q_col[n_q * ROWS :, :] = jnp.full((TILE, 128), -3.0, jnp.float32)
    for i in range(n_k):
        _, dx, dy, flip = keys[i]
        source = (((chip_y - dy) % SIDE) * SIDE + (chip_x - dx) % SIDE) * 2 + (core + flip) % 2
        allowed = pattern_ref[group, source] > 0
        k_col[i * ROWS : (i + 1) * ROWS, :] = column(jnp.where(allowed, label(n_q + i), -1.0))
    found_rows[...] = jnp.full_like(found_rows, -1.0)
    to_scalar.wait()

    for o in range(OWNERS + 1):
        q_next[o] = 0
        k_next[o] = 0

    def count(i, table):
        for j in range(GROUP):
            o = own_s[i, j * TILE]
            table[o] = table[o] + 1

    def count_q(i, carry):
        count(i, q_next)
        return carry

    def count_k(i, carry):
        count(i, k_next)
        return carry

    lax.fori_loop(0, n_q, count_q, 0)
    lax.fori_loop(n_q, n_q + n_k, count_k, 0)
    q_total, k_total = jnp.int32(0), jnp.int32(0)
    for o in range(OWNERS + 1):
        q_here, k_here = q_next[o], k_next[o]
        q_next[o], k_next[o] = q_total, k_total
        k_base[o] = k_total
        q_total = q_total + (q_here + GROUP - 1) // GROUP * GROUP
        k_total = k_total + k_here

    def no_tile(t, carry):
        q_order[t] = n_q * GROUP
        return carry

    lax.fori_loop(0, blocks * GROUP, no_tile, 0, unroll=8)

    def put_q(i, carry):
        for j in range(GROUP):
            o = own_s[i, j * TILE]
            to = q_next[o]
            q_next[o] = to + 1
            q_order[to] = i * GROUP + j
            q_own_s[to // GROUP] = o
        return carry

    def put_k(i, carry):
        for j in range(GROUP):
            o = own_s[n_q + i, j * TILE]
            to = k_next[o]
            k_next[o] = to + 1
            k_order[to] = i * GROUP + j
        return carry

    lax.fori_loop(0, n_q, put_q, 0)
    lax.fori_loop(0, n_k, put_k, 0)

    def tile_rows(t):
        return pl.ds(pl.multiple_of(t * TILE, TILE), TILE)

    inside = lax.broadcasted_iota(jnp.int32, (TILE, 128), 0)

    def names(t, other):
        return inside + jnp.where(t < GROUP, t * TILE, other)

    for b in range(blocks):
        tiles = [q_order[b * GROUP + j] for j in range(GROUP)]
        col = jnp.concatenate([q_col[tile_rows(t), :] for t in tiles], axis=0)
        q_rows[b] = jnp.transpose(col)[0:1, :]
        name = jnp.concatenate([names(t, -(1 << 20)) for t in tiles], axis=0)
        q_names[b] = jnp.transpose(name.astype(jnp.float32))[0:1, :].astype(jnp.int32)
    pltpu.make_async_copy(q_raw, q_raw, sems.at[1]).wait()
    pltpu.make_async_copy(k_raw, k_raw, sems.at[2]).wait()

    def block_step(b, carry):
        owner = q_own_s[b]
        lo = k_base[owner]
        q_row, q_name = q_rows[b], q_names[b]
        acc[...] = jnp.full_like(acc, -1.0)
        q_at = [jnp.minimum(q_order[b * GROUP + j], n_q * GROUP - 1) for j in range(GROUP)]

        here = k_base[owner + 1] - lo

        def chunk_step(per, m):
            tiles = [
                k_order[jnp.minimum(lo + m * per + i, k_tiles - 1)] for i in range(per)
            ]
            block = jnp.concatenate([q_raw[tile_rows(t), :] for t in q_at], axis=0)
            scores = lax.dot_general(
                jnp.concatenate([k_raw[tile_rows(t), :] for t in tiles], axis=0), block,
                (((1,), (1,)), ((), ())), preferred_element_type=jnp.float32,
            )
            col = jnp.concatenate([k_col[tile_rows(t), :] for t in tiles], axis=0)
            name = jnp.concatenate([names(t, -(1 << 21)) for t in tiles], axis=0)
            for h in range(ROWS // 128):
                lanes = slice(h * 128, (h + 1) * 128)
                match = (col == q_row[:, lanes]) & (name != q_name[:, lanes])
                found = jnp.where(match, scores[:, lanes], -1.0)
                found = jnp.max(found.reshape(per * TILE // 8, 8, 128), axis=0)
                acc[:, lanes] = jnp.maximum(acc[:, lanes], found)

        def large_step(m, inner):
            chunk_step(large, m)
            return inner

        fits = here <= small

        @pl.when(fits)
        def _():
            chunk_step(small, 0)

        lax.fori_loop(0, jnp.where(fits, 0, (here + large - 1) // large), large_step, 0)
        found_rows[b] = jnp.max(acc[...], axis=0, keepdims=True)
        return carry

    lax.fori_loop(0, q_total // GROUP, block_step, 0)
    for b in range(blocks):
        done = column(found_rows[b])
        for j in range(GROUP):
            spread[tile_rows(q_order[b * GROUP + j]), :] = done[j * TILE : (j + 1) * TILE, :]
    for s in range(n_q):
        to = (depth - queries[s][2] + 2 * n_q) % n_q
        out_ref[to] = jnp.transpose(spread[s * ROWS : (s + 1) * ROWS, :])[0:1, :]


def compare(where, pattern, arrays, queries, keys):
    n_q, n_k = len(queries), len(keys)
    width = arrays[0].shape[1]
    blocks = n_q + OWNERS
    smem = pl.BlockSpec(memory_space=pltpu.SMEM)
    anywhere = pl.BlockSpec(memory_space=pl.ANY)
    slots = -(-(n_q + n_k) // 8) * 8
    return pl.pallas_call(
        functools.partial(compare_kernel, queries, keys),
        out_shape=jax.ShapeDtypeStruct((n_q, 1, ROWS), jnp.float32),
        in_specs=[smem] * 2 + [anywhere] * len(arrays),
        out_specs=pl.BlockSpec(memory_space=pltpu.VMEM),
        scratch_shapes=[
            pltpu.VMEM((n_q * ROWS, width), jnp.bfloat16),
            pltpu.VMEM((n_k * ROWS, width), jnp.bfloat16),
            pltpu.VMEM((n_q * ROWS + TILE, 128), jnp.float32),
            pltpu.VMEM((n_k * ROWS, 128), jnp.float32),
            pltpu.VMEM((8, ROWS), jnp.float32),
            pltpu.VMEM((n_q * ROWS + TILE, 128), jnp.float32),
            pltpu.VMEM((n_q + n_k, 8, ROWS), jnp.bfloat16),
            pltpu.VMEM((slots, ROWS), jnp.int32),
            pltpu.SMEM((slots, ROWS), jnp.int32),
            pltpu.SMEM((OWNERS + 1,), jnp.int32),
            pltpu.SMEM((OWNERS + 1,), jnp.int32),
            pltpu.SMEM((OWNERS + 1,), jnp.int32),
            pltpu.SMEM((blocks * GROUP,), jnp.int32),
            pltpu.SMEM((blocks,), jnp.int32),
            pltpu.SMEM((n_k * GROUP,), jnp.int32),
            pltpu.SemaphoreType.DMA((3,)),
            pltpu.VMEM((blocks, 1, ROWS), jnp.float32),
            pltpu.VMEM((blocks, 1, ROWS), jnp.int32),
            pltpu.VMEM((blocks, 1, ROWS), jnp.float32),
        ],
        cost_estimate=pl.CostEstimate(
            flops=2 * n_q * n_k * ROWS * ROWS * width // 4,
            bytes_accessed=(n_q + n_k) * ROWS * width * 2,
            transcendentals=0,
        ),
        name="compare",
    )(where, pattern, *arrays)


def search(embeddings, cluster_ids, owners, pattern):
    n_own = lax.axis_size("own")
    tiles_here, tile_rows, width = embeddings.shape
    where = jnp.stack([lax.axis_index("grp"), lax.axis_index("own")]).astype(jnp.int32)

    labels = jnp.stack([cluster_ids, jnp.broadcast_to(owners, cluster_ids.shape)])
    labels = labels.reshape(2, ROWS).astype(jnp.bfloat16)
    labels = jnp.pad(labels, ((0, 6), (0, width - ROWS)))
    shard = jnp.concatenate([unit_rows(embeddings).reshape(ROWS, width), labels], axis=0)

    up, down = [shard], [shard]
    arrays = [shard]
    queries = [(0, 0, 0)]
    for hop in range(1, n_own // 2):
        up.append(along(up[-1], 1, n_own))
        down.append(along(down[-1], -1, n_own))
        at = len(arrays)
        queries += [(at, at, hop), (at + 1, at + 1, -hop)]
        arrays += [up[-1], down[-1]]
    far_low = along(up[-1][: ROWS // 2], 1, n_own)
    far_high = along(down[-1][ROWS // 2 :], -1, n_own)
    queries.append((len(arrays), len(arrays) + 1, n_own // 2))
    arrays += [far_low, far_high]

    held = {(0, 0): shard}
    keys = [(0, 0, 0, 0), (len(arrays), 0, 0, 1)]
    arrays.append(other_core(shard))
    for source, (dx, dy) in TREE:
        node = wrap((source[0] + dx, source[1] + dy))
        held[node] = in_plane(held[wrap(source)], dx, dy)
        keys += [(len(arrays), *node, 0), (len(arrays) + 1, *node, 1)]
        arrays += [held[node], other_core(held[node])]
    best = compare(where, pattern, arrays, queries, keys)

    returned = lax.all_to_all(best, "own", split_axis=0, concat_axis=0, tiled=True)
    return jnp.max(returned, axis=0).reshape(tiles_here, tile_rows)


def solution(mesh):
    placed = (P(("grp", "own"), None, None), P(("grp", "own"), None), P(("grp", "own"), None), P())
    return jax.shard_map(
        search, mesh=mesh, in_specs=placed, out_specs=P(("grp", "own"), None), check_vma=False
    )
```

```python
import functools

import jax
import jax.numpy as jnp
from jax import lax
from jax.experimental import pallas as pl
from jax.experimental.pallas import tpu as pltpu
from jax.sharding import PartitionSpec as P


TILE = 32
GROUP = 8
ROWS = TILE * GROUP
CHUNKS = (26 * TILE, 34 * TILE)

TREE = (
    ((0, 0), (1, 0)),
    ((0, 0), (-1, 0)),
    ((0, 0), (0, 1)),
    ((0, 0), (0, -1)),
    ((0, 1), (1, 0)),
    ((0, -1), (-1, 0)),
    ((-1, 0), (0, 1)),
    ((1, 0), (0, -1)),
    ((1, 0), (1, 0)),
    ((-1, -1), (-1, 0)),
    ((0, 1), (0, 1)),
    ((1, -1), (0, -1)),
    ((1, 1), (1, 0)),
    ((-1, 1), (0, 1)),
    ((2, 3), (0, -1)),
)
SIDE = 4
OWNERS = 8
CLUSTERS = 4


def wrap(node):
    return (node[0] % SIDE, node[1] % SIDE)


def plane_pairs(dx, dy, flip):
    pairs = []
    for y in range(SIDE):
        for x in range(SIDE):
            for core in range(2):
                source = (y * SIDE + x) * 2 + core
                dest = (((y + dy) % SIDE) * SIDE + (x + dx) % SIDE) * 2 + (core ^ flip)
                pairs.append((source, dest))
    return pairs


def in_plane(value, dx, dy):
    return lax.ppermute(value, "grp", plane_pairs(dx, dy, 0))


def other_core(value):
    return lax.ppermute(value, "grp", plane_pairs(0, 0, 1))


def along(value, step, count):
    return lax.ppermute(value, "own", [(i, (i + step) % count) for i in range(count)])


def unit_rows(values):
    wide = values.astype(jnp.float32)
    return (wide * lax.rsqrt(jnp.sum(wide * wide, axis=-1, keepdims=True) + 1e-06)).astype(
        jnp.bfloat16
    )


def compare_kernel(queries, keys, where_ref, pattern_ref, *refs):
    n_ops = max([h for _, h, _ in queries] + [k[0] for k in keys]) + 1
    arrays = refs[:n_ops]
    out_ref, q_raw, k_raw, q_col, k_col, acc, spread, meta, own_vec = refs[n_ops : n_ops + 9]
    own_s, k_base, q_next, k_next, q_order, q_own_s, k_order, sems = refs[n_ops + 9 : n_ops + 17]
    q_rows, q_names, found_rows, allow_s = refs[n_ops + 17 :]
    n_q, n_k = len(queries), len(keys)
    blocks = n_q + OWNERS
    small, large = (chunk // TILE for chunk in CHUNKS)
    half = ROWS // 2
    group, depth = where_ref[0], where_ref[1]
    chip_y, chip_x, core = group // (2 * SIDE), (group // 2) % SIDE, group % 2

    for i in range(n_q + n_k):
        if i < n_q:
            low, high, _ = queries[i]
            row = ROWS if low == high else half
        else:
            high, row = keys[i - n_q][0], ROWS
        pltpu.make_async_copy(
            arrays[high].at[pl.ds(row, 8), pl.ds(0, ROWS)], meta.at[i], sems.at[0]
        ).start()
    for i in range(n_q):
        low, high, _ = queries[i]
        if low == high:
            parts = [(low, i * ROWS, ROWS)]
        else:
            parts = [(low, i * ROWS, half), (high, i * ROWS + half, half)]
        for ref, to, rows in parts:
            pltpu.make_async_copy(
                arrays[ref].at[pl.ds(0, rows)], q_raw.at[pl.ds(to, rows)], sems.at[1]
            ).start()

    def key_copy(i):
        return pltpu.make_async_copy(
            arrays[keys[i][0]].at[pl.ds(0, ROWS)], k_raw.at[pl.ds(i * ROWS, ROWS)], sems.at[2 + i]
        )

    allows = []
    for i in range(n_k):
        _, dx, dy, flip = keys[i]
        source = (((chip_y - dy) % SIDE) * SIDE + (chip_x - dx) % SIDE) * 2 + (core + flip) % 2
        allows.append(pattern_ref[group, source])
        allow_s[i] = allows[i]

        @pl.when(allows[i] > 0)
        def _(i=i):
            key_copy(i).start()

    pltpu.make_async_copy(meta, meta, sems.at[0]).wait()
    for i in range(n_q + n_k):
        own_vec[i : i + 1, :] = meta[i].astype(jnp.float32)[1:2, :].astype(jnp.int32)
    to_scalar = pltpu.make_async_copy(own_vec, own_s, sems.at[0])
    to_scalar.start()

    def column(row):
        return jnp.transpose(jnp.broadcast_to(row, (128, ROWS)))

    def label(i):
        info = meta[i].astype(jnp.float32)
        return info[1:2, :] * CLUSTERS + info[0:1, :]

    for i in range(n_q):
        q_col[i * ROWS : (i + 1) * ROWS, :] = column(label(i))
    q_col[n_q * ROWS :, :] = jnp.full((TILE, 128), -3.0, jnp.float32)
    for i in range(n_k):
        k_col[i * ROWS : (i + 1) * ROWS, :] = column(label(n_q + i))
    found_rows[...] = jnp.full_like(found_rows, -1.0)
    to_scalar.wait()

    for o in range(OWNERS + 1):
        q_next[o] = 0
        k_next[o] = 0

    def count(i, table):
        for j in range(GROUP):
            o = own_s[i, j * TILE]
            table[o] = table[o] + 1

    def count_q(i, carry):
        count(i, q_next)
        return carry

    def count_k(i, carry):
        @pl.when(allow_s[i - n_q] > 0)
        def _():
            count(i, k_next)

        return carry

    lax.fori_loop(0, n_q, count_q, 0)
    lax.fori_loop(n_q, n_q + n_k, count_k, 0)
    q_total, k_total = jnp.int32(0), jnp.int32(0)
    for o in range(OWNERS + 1):
        q_here, k_here = q_next[o], k_next[o]
        q_next[o], k_next[o] = q_total, k_total
        k_base[o] = k_total
        q_total = q_total + (q_here + GROUP - 1) // GROUP * GROUP
        k_total = k_total + k_here

    def no_tile(t, carry):
        q_order[t] = n_q * GROUP
        return carry

    lax.fori_loop(0, blocks * GROUP, no_tile, 0, unroll=8)

    def put_q(i, carry):
        for j in range(GROUP):
            o = own_s[i, j * TILE]
            to = q_next[o]
            q_next[o] = to + 1
            q_order[to] = i * GROUP + j
            q_own_s[to // GROUP] = o
        return carry

    def put_k(i, carry):
        @pl.when(allow_s[i] > 0)
        def _():
            for j in range(GROUP):
                o = own_s[n_q + i, j * TILE]
                to = k_next[o]
                k_next[o] = to + 1
                k_order[to] = i * GROUP + j

        return carry

    lax.fori_loop(0, n_q, put_q, 0)
    lax.fori_loop(0, n_k, put_k, 0)

    def tile_rows(t):
        return pl.ds(pl.multiple_of(t * TILE, TILE), TILE)

    inside = lax.broadcasted_iota(jnp.int32, (TILE, 128), 0)

    def names(t, other):
        return inside + jnp.where(t < GROUP, t * TILE, other)

    for b in range(blocks):
        tiles = [q_order[b * GROUP + j] for j in range(GROUP)]
        col = jnp.concatenate([q_col[tile_rows(t), :] for t in tiles], axis=0)
        q_rows[b] = jnp.transpose(col)[0:1, :]
        name = jnp.concatenate([names(t, -(1 << 20)) for t in tiles], axis=0)
        q_names[b] = jnp.transpose(name.astype(jnp.float32))[0:1, :].astype(jnp.int32)
    pltpu.make_async_copy(q_raw, q_raw, sems.at[1]).wait()
    for i in range(n_k):

        @pl.when(allows[i] > 0)
        def _(i=i):
            key_copy(i).wait()


    def block_step(b, carry):
        owner = q_own_s[b]
        lo = k_base[owner]
        q_row, q_name = q_rows[b], q_names[b]
        acc[...] = jnp.full_like(acc, -1.0)
        q_at = [jnp.minimum(q_order[b * GROUP + j], n_q * GROUP - 1) for j in range(GROUP)]

        here = k_base[owner + 1] - lo

        def chunk_step(per, m):
            tiles = [
                k_order[jnp.minimum(lo + m * per + i, k_total - 1)] for i in range(per)
            ]
            block = jnp.concatenate([q_raw[tile_rows(t), :] for t in q_at], axis=0)
            scores = lax.dot_general(
                jnp.concatenate([k_raw[tile_rows(t), :] for t in tiles], axis=0), block,
                (((1,), (1,)), ((), ())), preferred_element_type=jnp.float32,
            )
            col = jnp.concatenate([k_col[tile_rows(t), :] for t in tiles], axis=0)
            name = jnp.concatenate([names(t, -(1 << 21)) for t in tiles], axis=0)
            for h in range(ROWS // 128):
                lanes = slice(h * 128, (h + 1) * 128)
                match = (col == q_row[:, lanes]) & (name != q_name[:, lanes])
                found = jnp.where(match, scores[:, lanes], -1.0)
                found = jnp.max(found.reshape(per * TILE // 8, 8, 128), axis=0)
                acc[:, lanes] = jnp.maximum(acc[:, lanes], found)

        def large_step(m, inner):
            chunk_step(large, m)
            return inner

        fits = here <= small

        @pl.when(fits & (here > 0))
        def _():
            chunk_step(small, 0)

        lax.fori_loop(0, jnp.where(fits, 0, (here + large - 1) // large), large_step, 0)
        found_rows[b] = jnp.max(acc[...], axis=0, keepdims=True)
        return carry

    lax.fori_loop(0, q_total // GROUP, block_step, 0)
    for b in range(blocks):
        done = column(found_rows[b])
        for j in range(GROUP):
            spread[tile_rows(q_order[b * GROUP + j]), :] = done[j * TILE : (j + 1) * TILE, :]
    for s in range(n_q):
        to = (depth - queries[s][2] + 2 * n_q) % n_q
        out_ref[to] = jnp.transpose(spread[s * ROWS : (s + 1) * ROWS, :])[0:1, :]


def compare(where, pattern, arrays, queries, keys):
    n_q, n_k = len(queries), len(keys)
    width = arrays[0].shape[1]
    blocks = n_q + OWNERS
    smem = pl.BlockSpec(memory_space=pltpu.SMEM)
    anywhere = pl.BlockSpec(memory_space=pl.ANY)
    slots = -(-(n_q + n_k) // 8) * 8
    return pl.pallas_call(
        functools.partial(compare_kernel, queries, keys),
        out_shape=jax.ShapeDtypeStruct((n_q, 1, ROWS), jnp.float32),
        in_specs=[smem] * 2 + [anywhere] * len(arrays),
        out_specs=pl.BlockSpec(memory_space=pltpu.VMEM),
        scratch_shapes=[
            pltpu.VMEM((n_q * ROWS, width), jnp.bfloat16),
            pltpu.VMEM((n_k * ROWS, width), jnp.bfloat16),
            pltpu.VMEM((n_q * ROWS + TILE, 128), jnp.float32),
            pltpu.VMEM((n_k * ROWS, 128), jnp.float32),
            pltpu.VMEM((8, ROWS), jnp.float32),
            pltpu.VMEM((n_q * ROWS + TILE, 128), jnp.float32),
            pltpu.VMEM((n_q + n_k, 8, ROWS), jnp.bfloat16),
            pltpu.VMEM((slots, ROWS), jnp.int32),
            pltpu.SMEM((slots, ROWS), jnp.int32),
            pltpu.SMEM((OWNERS + 1,), jnp.int32),
            pltpu.SMEM((OWNERS + 1,), jnp.int32),
            pltpu.SMEM((OWNERS + 1,), jnp.int32),
            pltpu.SMEM((blocks * GROUP,), jnp.int32),
            pltpu.SMEM((blocks,), jnp.int32),
            pltpu.SMEM((n_k * GROUP,), jnp.int32),
            pltpu.SemaphoreType.DMA((2 + n_k,)),
            pltpu.VMEM((blocks, 1, ROWS), jnp.float32),
            pltpu.VMEM((blocks, 1, ROWS), jnp.int32),
            pltpu.VMEM((blocks, 1, ROWS), jnp.float32),
            pltpu.SMEM((n_k,), jnp.int32),
        ],
        cost_estimate=pl.CostEstimate(
            flops=2 * n_q * n_k * ROWS * ROWS * width // 4,
            bytes_accessed=(n_q + n_k) * ROWS * width * 2,
            transcendentals=0,
        ),
        name="compare",
    )(where, pattern, *arrays)


def search(embeddings, cluster_ids, owners, pattern):
    n_own = lax.axis_size("own")
    tiles_here, tile_rows, width = embeddings.shape
    where = jnp.stack([lax.axis_index("grp"), lax.axis_index("own")]).astype(jnp.int32)

    labels = jnp.stack([cluster_ids, jnp.broadcast_to(owners, cluster_ids.shape)])
    labels = labels.reshape(2, ROWS).astype(jnp.bfloat16)
    labels = jnp.pad(labels, ((0, 6), (0, width - ROWS)))
    shard = jnp.concatenate([unit_rows(embeddings).reshape(ROWS, width), labels], axis=0)

    up, down = [shard], [shard]
    arrays = [shard]
    queries = [(0, 0, 0)]
    last, half = n_own // 2, ROWS // 2
    for hop in range(1, last - 1):
        up.append(along(up[-1], 1, n_own))
        down.append(along(down[-1], -1, n_own))
        at = len(arrays)
        queries += [(at, at, hop), (at + 1, at + 1, -hop)]
        arrays += [up[-1], down[-1]]
    up_low = along(up[-1][:half], 1, n_own)
    down_high = along(down[-1][half:], -1, n_own)
    up_high = along(up[-1][half:], 1, n_own)
    down_low = along(down[-1][:half], -1, n_own)
    far_low = along(up_low, 1, n_own)
    far_high = along(down_high, -1, n_own)
    for low, high, step in (
        (up_low, up_high, last - 1), (down_low, down_high, 1 - last), (far_low, far_high, last)
    ):
        queries.append((len(arrays), len(arrays) + 1, step))
        arrays += [low, high]

    held = {(0, 0): shard}
    keys = [(0, 0, 0, 0), (len(arrays), 0, 0, 1)]
    arrays.append(other_core(shard))
    for source, (dx, dy) in TREE:
        node = wrap((source[0] + dx, source[1] + dy))
        held[node] = in_plane(held[wrap(source)], dx, dy)
        keys += [(len(arrays), *node, 0), (len(arrays) + 1, *node, 1)]
        arrays += [held[node], other_core(held[node])]
    best = compare(where, pattern, arrays, queries, keys)

    returned = lax.all_to_all(best, "own", split_axis=0, concat_axis=0, tiled=True)
    return jnp.max(returned, axis=0).reshape(tiles_here, tile_rows)


def solution(mesh):
    placed = (P(("grp", "own"), None, None), P(("grp", "own"), None), P(("grp", "own"), None), P())
    return jax.shard_map(
        search, mesh=mesh, in_specs=placed, out_specs=P(("grp", "own"), None), check_vma=False
    )
```

```python
import functools

import jax
import jax.numpy as jnp
from jax import lax
from jax.experimental import pallas as pl
from jax.experimental.pallas import tpu as pltpu
from jax.sharding import PartitionSpec as P


TILE = 32
GROUP = 8
ROWS = TILE * GROUP
CHUNKS = (26 * TILE, 34 * TILE)

TREE = (
    ((0, 0), (1, 0)),
    ((0, 0), (-1, 0)),
    ((0, 0), (0, 1)),
    ((0, 0), (0, -1)),
    ((0, 1), (1, 0)),
    ((0, -1), (-1, 0)),
    ((-1, 0), (0, 1)),
    ((1, 0), (0, -1)),
    ((1, 0), (1, 0)),
    ((-1, -1), (-1, 0)),
    ((0, 1), (0, 1)),
    ((1, -1), (0, -1)),
    ((1, 1), (1, 0)),
    ((-1, 1), (0, 1)),
    ((2, 3), (0, -1)),
)
SIDE = 4
OWNERS = 8
CLUSTERS = 4


def wrap(node):
    return (node[0] % SIDE, node[1] % SIDE)


def plane_pairs(dx, dy, flip):
    pairs = []
    for y in range(SIDE):
        for x in range(SIDE):
            for core in range(2):
                source = (y * SIDE + x) * 2 + core
                dest = (((y + dy) % SIDE) * SIDE + (x + dx) % SIDE) * 2 + (core ^ flip)
                pairs.append((source, dest))
    return pairs


def in_plane(value, dx, dy):
    return lax.ppermute(value, "grp", plane_pairs(dx, dy, 0))


def other_core(value):
    return lax.ppermute(value, "grp", plane_pairs(0, 0, 1))


def along(value, step, count):
    return lax.ppermute(value, "own", [(i, (i + step) % count) for i in range(count)])


def unit_rows(values):
    wide = values.astype(jnp.float32)
    return (wide * lax.rsqrt(jnp.sum(wide * wide, axis=-1, keepdims=True) + 1e-06)).astype(
        jnp.bfloat16
    )


def compare_kernel(queries, keys, where_ref, pattern_ref, *refs):
    n_ops = max([h for _, h, _ in queries] + [k[0] for k in keys]) + 1
    arrays = refs[:n_ops]
    out_ref, q_raw, k_raw, q_col, k_col, acc, spread, meta, own_vec = refs[n_ops : n_ops + 9]
    own_s, k_base, q_next, k_next, q_order, q_own_s, k_order, sems = refs[n_ops + 9 : n_ops + 17]
    q_rows, q_names, found_rows, allow_s = refs[n_ops + 17 :]
    n_q, n_k = len(queries), len(keys)
    blocks = n_q + OWNERS
    small, large = (chunk // TILE for chunk in CHUNKS)
    half = ROWS // 2
    group, depth = where_ref[0], where_ref[1]
    chip_y, chip_x, core = group // (2 * SIDE), (group // 2) % SIDE, group % 2

    for i in range(n_q + n_k):
        if i < n_q:
            low, high, _ = queries[i]
            row = ROWS if low == high else half
        else:
            high, row = keys[i - n_q][0], ROWS
        pltpu.make_async_copy(
            arrays[high].at[pl.ds(row, 8), pl.ds(0, ROWS)], meta.at[i], sems.at[0]
        ).start()
    for i in range(n_q):
        low, high, _ = queries[i]
        if low == high:
            parts = [(low, i * ROWS, ROWS)]
        else:
            parts = [(low, i * ROWS, half), (high, i * ROWS + half, half)]
        for ref, to, rows in parts:
            pltpu.make_async_copy(
                arrays[ref].at[pl.ds(0, rows)], q_raw.at[pl.ds(to, rows)], sems.at[1]
            ).start()

    def key_copy(i):
        return pltpu.make_async_copy(
            arrays[keys[i][0]].at[pl.ds(0, ROWS)], k_raw.at[pl.ds(i * ROWS, ROWS)], sems.at[2 + i]
        )

    allows = []
    for i in range(n_k):
        _, dx, dy, flip = keys[i]
        source = (((chip_y - dy) % SIDE) * SIDE + (chip_x - dx) % SIDE) * 2 + (core + flip) % 2
        allows.append(pattern_ref[group, source])
        allow_s[i] = allows[i]

        @pl.when(allows[i] > 0)
        def _(i=i):
            key_copy(i).start()

    pltpu.make_async_copy(meta, meta, sems.at[0]).wait()
    for i in range(n_q + n_k):
        own_vec[i : i + 1, :] = meta[i].astype(jnp.float32)[1:2, :].astype(jnp.int32)
    to_scalar = pltpu.make_async_copy(own_vec, own_s, sems.at[0])
    to_scalar.start()

    def column(row):
        return jnp.transpose(jnp.broadcast_to(row, (128, ROWS)))

    def label(i):
        info = meta[i].astype(jnp.float32)
        return info[1:2, :] * CLUSTERS + info[0:1, :]

    for i in range(n_q):
        q_col[i * ROWS : (i + 1) * ROWS, :] = column(label(i))
    q_col[n_q * ROWS :, :] = jnp.full((TILE, 128), -3.0, jnp.float32)
    for i in range(n_k):
        k_col[i * ROWS : (i + 1) * ROWS, :] = column(label(n_q + i))
    found_rows[...] = jnp.full_like(found_rows, -1.0)
    to_scalar.wait()

    for o in range(OWNERS + 1):
        q_next[o] = 0
        k_next[o] = 0

    def count(i, table):
        for j in range(GROUP):
            o = own_s[i, j * TILE]
            table[o] = table[o] + 1

    def count_q(i, carry):
        count(i, q_next)
        return carry

    def count_k(i, carry):
        @pl.when(allow_s[i - n_q] > 0)
        def _():
            count(i, k_next)

        return carry

    lax.fori_loop(0, n_q, count_q, 0)
    lax.fori_loop(n_q, n_q + n_k, count_k, 0)
    q_total, k_total = jnp.int32(0), jnp.int32(0)
    for o in range(OWNERS + 1):
        q_here, k_here = q_next[o], k_next[o]
        q_next[o], k_next[o] = q_total, k_total
        k_base[o] = k_total
        q_total = q_total + (q_here + GROUP - 1) // GROUP * GROUP
        k_total = k_total + k_here

    def no_tile(t, carry):
        q_order[t] = n_q * GROUP
        return carry

    lax.fori_loop(0, blocks * GROUP, no_tile, 0, unroll=8)

    def put_q(i, carry):
        for j in range(GROUP):
            o = own_s[i, j * TILE]
            to = q_next[o]
            q_next[o] = to + 1
            q_order[to] = i * GROUP + j
            q_own_s[to // GROUP] = o
        return carry

    def put_k(i, carry):
        @pl.when(allow_s[i] > 0)
        def _():
            for j in range(GROUP):
                o = own_s[n_q + i, j * TILE]
                to = k_next[o]
                k_next[o] = to + 1
                k_order[to] = i * GROUP + j

        return carry

    lax.fori_loop(0, n_q, put_q, 0)
    lax.fori_loop(0, n_k, put_k, 0)

    def tile_rows(t):
        return pl.ds(pl.multiple_of(t * TILE, TILE), TILE)

    inside = lax.broadcasted_iota(jnp.int32, (TILE, 128), 0)

    def names(t, other):
        return inside + jnp.where(t < GROUP, t * TILE, other)

    for b in range(blocks):
        tiles = [q_order[b * GROUP + j] for j in range(GROUP)]
        col = jnp.concatenate([q_col[tile_rows(t), :] for t in tiles], axis=0)
        q_rows[b] = jnp.transpose(col)[0:1, :]
        name = jnp.concatenate([names(t, -(1 << 20)) for t in tiles], axis=0)
        q_names[b] = jnp.transpose(name.astype(jnp.float32))[0:1, :].astype(jnp.int32)
    pltpu.make_async_copy(q_raw, q_raw, sems.at[1]).wait()
    for i in range(n_k):

        @pl.when(allows[i] > 0)
        def _(i=i):
            key_copy(i).wait()


    def block_step(b, carry):
        owner = q_own_s[b]
        lo = k_base[owner]
        q_row, q_name = q_rows[b], q_names[b]
        acc[...] = jnp.full_like(acc, -1.0)
        q_at = [jnp.minimum(q_order[b * GROUP + j], n_q * GROUP - 1) for j in range(GROUP)]

        here = k_base[owner + 1] - lo

        def chunk_step(per, m):
            tiles = [
                k_order[jnp.minimum(lo + m * per + i, k_total - 1)] for i in range(per)
            ]
            block = jnp.concatenate([q_raw[tile_rows(t), :] for t in q_at], axis=0)
            scores = lax.dot_general(
                jnp.concatenate([k_raw[tile_rows(t), :] for t in tiles], axis=0), block,
                (((1,), (1,)), ((), ())), preferred_element_type=jnp.float32,
            )
            col = jnp.concatenate([k_col[tile_rows(t), :] for t in tiles], axis=0)
            name = jnp.concatenate([names(t, -(1 << 21)) for t in tiles], axis=0)
            for h in range(ROWS // 128):
                lanes = slice(h * 128, (h + 1) * 128)
                match = (col == q_row[:, lanes]) & (name != q_name[:, lanes])
                found = jnp.where(match, scores[:, lanes], -1.0)
                found = jnp.max(found.reshape(per * TILE // 8, 8, 128), axis=0)
                acc[:, lanes] = jnp.maximum(acc[:, lanes], found)

        def large_step(m, inner):
            chunk_step(large, m)
            return inner

        fits = here <= small

        @pl.when(fits & (here > 0))
        def _():
            chunk_step(small, 0)

        lax.fori_loop(0, jnp.where(fits, 0, (here + large - 1) // large), large_step, 0)
        found_rows[b] = jnp.max(acc[...], axis=0, keepdims=True)
        return carry

    lax.fori_loop(0, q_total // GROUP, block_step, 0)
    for b in range(blocks):
        done = column(found_rows[b])
        for j in range(GROUP):
            spread[tile_rows(q_order[b * GROUP + j]), :] = done[j * TILE : (j + 1) * TILE, :]
    for s in range(n_q):
        to = (depth - queries[s][2] + 2 * n_q) % n_q
        out_ref[to] = jnp.transpose(spread[s * ROWS : (s + 1) * ROWS, :])[0:1, :]


def compare(where, pattern, arrays, queries, keys):
    n_q, n_k = len(queries), len(keys)
    width = arrays[0].shape[1]
    blocks = n_q + OWNERS
    smem = pl.BlockSpec(memory_space=pltpu.SMEM)
    anywhere = pl.BlockSpec(memory_space=pl.ANY)
    slots = -(-(n_q + n_k) // 8) * 8
    return pl.pallas_call(
        functools.partial(compare_kernel, queries, keys),
        out_shape=jax.ShapeDtypeStruct((n_q, 1, ROWS), jnp.float32),
        in_specs=[smem] * 2 + [anywhere] * len(arrays),
        out_specs=pl.BlockSpec(memory_space=pltpu.VMEM),
        scratch_shapes=[
            pltpu.VMEM((n_q * ROWS, width), jnp.bfloat16),
            pltpu.VMEM((n_k * ROWS, width), jnp.bfloat16),
            pltpu.VMEM((n_q * ROWS + TILE, 128), jnp.float32),
            pltpu.VMEM((n_k * ROWS, 128), jnp.float32),
            pltpu.VMEM((8, ROWS), jnp.float32),
            pltpu.VMEM((n_q * ROWS + TILE, 128), jnp.float32),
            pltpu.VMEM((n_q + n_k, 8, ROWS), jnp.bfloat16),
            pltpu.VMEM((slots, ROWS), jnp.int32),
            pltpu.SMEM((slots, ROWS), jnp.int32),
            pltpu.SMEM((OWNERS + 1,), jnp.int32),
            pltpu.SMEM((OWNERS + 1,), jnp.int32),
            pltpu.SMEM((OWNERS + 1,), jnp.int32),
            pltpu.SMEM((blocks * GROUP,), jnp.int32),
            pltpu.SMEM((blocks,), jnp.int32),
            pltpu.SMEM((n_k * GROUP,), jnp.int32),
            pltpu.SemaphoreType.DMA((2 + n_k,)),
            pltpu.VMEM((blocks, 1, ROWS), jnp.float32),
            pltpu.VMEM((blocks, 1, ROWS), jnp.int32),
            pltpu.VMEM((blocks, 1, ROWS), jnp.float32),
            pltpu.SMEM((n_k,), jnp.int32),
        ],
        cost_estimate=pl.CostEstimate(
            flops=2 * n_q * n_k * ROWS * ROWS * width // 4,
            bytes_accessed=(n_q + n_k) * ROWS * width * 2,
            transcendentals=0,
        ),
        name="compare",
    )(where, pattern, *arrays)


def search(embeddings, cluster_ids, owners, pattern):
    n_own = lax.axis_size("own")
    tiles_here, tile_rows, width = embeddings.shape
    where = jnp.stack([lax.axis_index("grp"), lax.axis_index("own")]).astype(jnp.int32)

    labels = jnp.stack([cluster_ids, jnp.broadcast_to(owners, cluster_ids.shape)])
    labels = labels.reshape(2, ROWS).astype(jnp.bfloat16)
    labels = jnp.pad(labels, ((0, 6), (0, width - ROWS)))
    shard = jnp.concatenate([unit_rows(embeddings).reshape(ROWS, width), labels], axis=0)

    up, down = [shard], [shard]
    arrays = [shard]
    queries = [(0, 0, 0)]
    for hop in range(1, n_own // 2):
        up.append(along(up[-1], 1, n_own))
        down.append(along(down[-1], -1, n_own))
        at = len(arrays)
        queries += [(at, at, hop), (at + 1, at + 1, -hop)]
        arrays += [up[-1], down[-1]]
    far_low = along(up[-1][: ROWS // 2], 1, n_own)
    far_high = along(down[-1][ROWS // 2 :], -1, n_own)
    queries.append((len(arrays), len(arrays) + 1, n_own // 2))
    arrays += [far_low, far_high]

    held = {(0, 0): shard}
    keys = [(0, 0, 0, 0), (len(arrays), 0, 0, 1)]
    arrays.append(other_core(shard))
    for source, (dx, dy) in TREE:
        node = wrap((source[0] + dx, source[1] + dy))
        held[node] = in_plane(held[wrap(source)], dx, dy)
        keys += [(len(arrays), *node, 0), (len(arrays) + 1, *node, 1)]
        arrays += [held[node], other_core(held[node])]
    best = compare(where, pattern, arrays, queries, keys)

    returned = lax.all_to_all(best, "own", split_axis=0, concat_axis=0, tiled=True)
    return jnp.max(returned, axis=0).reshape(tiles_here, tile_rows)


def solution(mesh):
    placed = (P(("grp", "own"), None, None), P(("grp", "own"), None), P(("grp", "own"), None), P())
    return jax.shard_map(
        search, mesh=mesh, in_specs=placed, out_specs=P(("grp", "own"), None), check_vma=False
    )
```
